32 devices in a mesh: groups: 2 (over y), span: 4 (over x, core), head: 4 (over z).
Axes of the slice: x: 2, y: 2, z: 4, core: 2. Of those that a mesh axis runs over, the one named last changes fastest.
Arguments:
- queries: bfloat16 [4096, 1024], P(('groups', 'span', 'head')), parts along dimension 0, may hold values from -8 to 8
- keys: bfloat16 [4096, 1024], P(('groups', 'span', 'head')), parts along dimension 0, may hold values from -8 to 8
- values: bfloat16 [4096, 1024], P(('groups', 'span', 'head')), parts along dimension 0, may hold values from -6 to 6
- tile_offsets: int32 [32, 7], P(('groups', 'span')), parts along dimension 0, may hold values from 0 to 6, as said below
- timesteps: int32 [8], P(('groups', 'span')), parts along dimension 0, may hold values from 0 to 999
- time_weight: bfloat16 [256, 1024], P(None, 'head'), may hold values from -0.375 to 0.375
Outputs:
- attended: bfloat16 [4096, 1024], P(('groups', 'span', 'head')), parts along dimension 0
The draws below stay inside these ranges and needn't reach their ends.
There are 2 independent parts, one for each index of `groups`. The reference program is written for one: setup_inputs(seed, part) draws one part's arguments, and reference() takes and returns one part's arrays. A program takes and returns all parts, laid end to end along the dimension named above; an argument that names none is the same for every part. Nothing has to cross between parts.
Inputs may be any that keep to these rules, and one draw needn't show every extreme that they name: `tile_offsets`: the first entry of each row is 0 and the 7 entries of a row are distinct.
All inputs are finite; a program needn't handle non-finite values.
Results may differ from the reference program's by a relative error of at most 0.0035.
Values may be sent and summed in bfloat16 or wider, within the bound.
No kernel may reach another device: no remote copies, remote signals or barrier semaphores. Data moves between devices by JAX's collectives and lax.ppermute only.
A program may use at most 64 MiB of HBM per device.

```python
import math
import jax
import jax.numpy as jnp
from jax import lax

HEAD_SIZE = 128
TILE = 128
FREQ = 256
HEADS = 8
SPANS = 4
TOKENS = 2048
QT = 4
TILES = 16
REACH = 6
KT = 7


def base_field(key):
    width = HEADS * HEAD_SIZE
    return 1.414 * jax.random.truncated_normal(key, -5.5, 5.5, (TOKENS, width), jnp.float32)


def draw_queries(key, part):
    field = base_field(jax.random.fold_in(key, 11))
    return field.astype(jnp.bfloat16)


def draw_keys(key, part):
    field = base_field(jax.random.fold_in(key, 23))
    return field.astype(jnp.bfloat16)


def draw_tile_offsets(key, part):
    scores = jax.random.randint(jax.random.fold_in(key, 37), (TILES, REACH), 0, 1 << 20, dtype=jnp.int32)
    scores = scores * REACH + jnp.arange(REACH, dtype=jnp.int32)[None, :]
    order = jnp.argsort(scores, axis=1).astype(jnp.int32)
    picked = order[:, :KT - 1] + 1
    first = jnp.zeros((TILES, 1), jnp.int32)
    return jnp.concatenate([first, picked], axis=1).astype(jnp.int32)


def set_ends(values, key, low, top_value):
    longest = values.shape.index(max(values.shape))
    spots = []
    for shift in (0, 1):
        where = [jax.random.randint(jax.random.fold_in(key, axis), (), 0, length) for axis, length in enumerate(values.shape)]
        where[longest] = (where[longest] + shift) % values.shape[longest]
        spots.append(tuple(where))
    return values.at[spots[0]].set(low).at[spots[1]].set(top_value)


def levels(rng, dims, pieces, low, top_value):
    def one(dim, shards_of):
        heights = jax.random.uniform(jax.random.fold_in(jax.random.fold_in(rng, 6), dim), (shards_of,), jnp.float32, low / len(pieces), top_value / len(pieces))
        return jnp.repeat(jnp.exp(heights), dims[dim] // shards_of).reshape((-1,) + (1,) * (len(dims) - dim - 1))

    loudness = one(*pieces[0])
    for cut in pieces[1:]:
        loudness = loudness * one(*cut)
    return loudness


def noise(own_key, dims, spread, bound, cuts=(), kind=jnp.bfloat16):
    gain = levels(own_key, dims, cuts, -0.22, 0.18) if cuts else 1.0
    array = jax.random.normal(own_key, dims, jnp.float32) * spread * gain
    return jnp.minimum(jnp.maximum(array, -bound), bound).astype(kind)


def setup_inputs(seed: int = 0, part: int = 0) -> dict:
    key_list = jax.random.split(jax.random.key(seed), 7)
    part_splits = jax.random.split(jax.random.fold_in(key_list[6], part), 7)
    return {
        "queries": draw_queries(jax.random.fold_in(jax.random.fold_in(key_list[6], part), 71), part),
        "keys": draw_keys(jax.random.fold_in(jax.random.fold_in(key_list[6], part), 71), part),
        "values": noise(part_splits[2], (TOKENS, HEADS * HEAD_SIZE), 1.0, 6.0, ((0, 16),)),
        "tile_offsets": draw_tile_offsets(jax.random.fold_in(jax.random.fold_in(key_list[6], part), 71), part),
        "timesteps": set_ends(jax.random.randint(part_splits[4], (SPANS,), 0, 1000), jax.random.fold_in(part_splits[4], 1), 0, 999).astype(jnp.int32),
        "time_weight": noise(key_list[5], (FREQ, HEADS * HEAD_SIZE), FREQ ** -0.5, 0.375, ((1, 4),)),
    }


def timestep_gate(timesteps, time_weight):
    half = FREQ // 2
    freqs = jnp.exp(-math.log(10000.0) * jnp.arange(half, dtype=jnp.float32) / half)
    angles = timesteps.astype(jnp.float32)[:, None] * freqs[None, :]
    embedded = jnp.concatenate([jnp.cos(angles), jnp.sin(angles)], axis=1)
    return jnp.dot(embedded, time_weight.astype(jnp.float32), precision=lax.Precision.HIGHEST)


def reference(queries, keys, values, tile_offsets, timesteps, time_weight):
    width = HEADS * HEAD_SIZE
    gate = timestep_gate(timesteps, time_weight)
    padding = jnp.zeros((REACH * TILE, width), jnp.bfloat16)
    key_tiles = jnp.concatenate([padding, keys], axis=0).reshape(REACH + TILES, TILE, width)
    value_tiles = jnp.concatenate([padding, values], axis=0).reshape(REACH + TILES, TILE, width)
    query_blocks = queries.reshape(TILES // 4, 4, TILE, HEADS, HEAD_SIZE)
    offset_blocks = tile_offsets.reshape(TILES // 4, 4, KT)
    scale = HEAD_SIZE ** -0.5

    def one_block(inputs):
        block, query_part, offsets = inputs
        tiles_now = block * 4 + jnp.arange(4, dtype=jnp.int32)
        source = tiles_now[:, None] - offsets
        usable = source >= 0
        index = (source + REACH).astype(jnp.int32)
        key_part = key_tiles[index].reshape(4, KT * TILE, HEADS, HEAD_SIZE).astype(jnp.float32)
        value_part = value_tiles[index].reshape(4, KT * TILE, HEADS, HEAD_SIZE).astype(jnp.float32)
        scores = jnp.einsum("qthd,qkhd->qhtk", query_part.astype(jnp.float32), key_part) * scale
        keep = jnp.repeat(usable, TILE, axis=1)
        scores = jnp.where(keep[:, None, None, :], scores, -1e30)
        top = jnp.max(scores, axis=-1, keepdims=True)
        weights = jnp.exp(scores - top)
        total = jnp.sum(weights, axis=-1, keepdims=True)
        rounded = lax.optimization_barrier(weights.astype(jnp.bfloat16)).astype(jnp.float32)
        mixed = jnp.einsum("qhtk,qkhd->qthd", rounded, value_part)
        mixed = mixed / jnp.transpose(total, (0, 2, 1, 3))
        span_of = tiles_now // QT
        gate_rows = gate[span_of].reshape(4, 1, HEADS, HEAD_SIZE)
        return (mixed * (1.0 + gate_rows)).astype(jnp.bfloat16)

    blocks = jnp.arange(TILES // 4, dtype=jnp.int32)
    result = lax.map(one_block, (blocks, query_blocks, offset_blocks))
    return result.reshape(TOKENS, width)
```

```python
import functools
import math

import jax
import jax.numpy as jnp
from jax import lax
from jax.experimental import pallas as pl
from jax.experimental.pallas import tpu as pltpu
from jax.sharding import PartitionSpec as P

HEAD_SIZE = 128
TILE = 128
FREQ = 256


def attend(shape, tile_step, where_ref, offsets_ref, gate_ref, q_ref, window_ref, out_ref):
    count, listed, tail = shape
    width = q_ref.shape[1]
    position, place = where_ref[0], where_ref[1]
    tile = jnp.bitwise_xor(place, tile_step)
    scale = HEAD_SIZE ** (-0.5)
    slots, usable = [], []
    for j in range(listed):
        source = tile - offsets_ref[tile, j]
        step = jnp.bitwise_xor(jnp.bitwise_and(source, count - 1), place)
        slots.append(
            jnp.where(
                source >= 0,
                tail + count + step,
                jnp.where(source >= -count, tail + step, jnp.bitwise_and(step, tail - 1)),
            )
        )
        usable.append(position * count + source >= 0)
    for h in range(width // HEAD_SIZE):
        cols = slice(h * HEAD_SIZE, (h + 1) * HEAD_SIZE)
        value_cols = slice(width + h * HEAD_SIZE, width + (h + 1) * HEAD_SIZE)
        q = q_ref[:, cols]
        scores = []
        for j in range(listed):
            s = lax.dot_general(
                q, window_ref[slots[j], :, cols], (((1,), (1,)), ((), ())),
                preferred_element_type=jnp.float32,
            )
            scores.append(jnp.where(usable[j], s * scale, -1e30))
        top = functools.reduce(jnp.maximum, scores)
        top = jnp.max(top, axis=1, keepdims=True)
        total = jnp.zeros((TILE, HEAD_SIZE), jnp.float32)
        mixed = jnp.zeros((TILE, HEAD_SIZE), jnp.float32)
        for j in range(listed):
            weights = jnp.exp(scores[j] - top)
            total = total + weights
            mixed = mixed + jnp.dot(
                weights.astype(jnp.bfloat16), window_ref[slots[j], :, value_cols],
                preferred_element_type=jnp.float32,
            )
        total = jnp.sum(total, axis=1, keepdims=True)
        out_ref[:, cols] = (mixed / total * (1.0 + gate_ref[:, cols])).astype(jnp.bfloat16)


def place_pieces(count, where_ref, *refs):
    pieces, out_ref, sems = refs[:count], refs[count], refs[count + 1]
    width = pieces[0].shape[1]
    copies = []
    for step in range(count):
        column = pl.multiple_of(jnp.bitwise_xor(where_ref[1], step) * width, width)
        copies.append(
            pltpu.make_async_copy(pieces[step], out_ref.at[:, pl.ds(column, width)], sems.at[step])
        )
        copies[-1].start()
    for copy in copies:
        copy.wait()


SMEM = pl.BlockSpec(memory_space=pltpu.SMEM)
VMEM = pl.BlockSpec(memory_space=pltpu.VMEM)


def local(queries, keys, values, tile_offsets, timesteps, time_weight):
    count = lax.axis_size("head")
    spans = lax.axis_size("span")
    rows, channels = queries.shape
    width = channels // count
    listed = tile_offsets.shape[1]
    half_count = count // 2
    position, place = lax.axis_index("span"), lax.axis_index("head")
    where = jnp.stack([position, place]).astype(jnp.int32)

    def piece(array, step):
        return lax.dynamic_slice(array, (0, (place ^ step) * width), (rows, width))

    def swap(value, step):
        return lax.ppermute(value, "head", [(i, i ^ step) for i in range(count)])

    far_first = list(range(half_count, count)) + list(range(half_count - 1, 0, -1))
    held = {0: jnp.concatenate([piece(keys, 0), piece(values, 0)], axis=1)}
    for step in far_first:
        held[step] = swap(jnp.concatenate([piece(keys, step), piece(values, step)], axis=1), step)
    asked = {0: piece(queries, 0)}
    for step in far_first:
        asked[step] = swap(piece(queries, step), step)

    quarter = max(count // 4, 1)
    groups = [
        list(range(half_count)),
        list(range(half_count, half_count + quarter)),
        list(range(half_count + quarter, count)),
    ]
    near, far_low, far_high = [], [], []
    own = []
    for group in groups:
        stacked = jnp.stack([held[step] for step in group])
        own.append(stacked)
        near.append(lax.ppermute(stacked, "span", [(i, i + 1) for i in range(spans - 1)]))
        low = group[0] < half_count
        pairs = [
            (i * count + z, (i + 2) * count + z)
            for i in range(spans - 2)
            for z in range(count)
            if (z >= half_count) == low
        ]
        (far_low if low else far_high).append(lax.ppermute(stacked, ("span", "head"), pairs))
    far = jnp.where(place >= half_count, jnp.concatenate(far_low), jnp.concatenate(far_high))
    window = jnp.concatenate([far] + near + own, axis=0)

    half = FREQ // 2
    freqs = jnp.exp(-math.log(10000.0) * jnp.arange(half, dtype=jnp.float32) / half)
    angles = timesteps.astype(jnp.float32)[:, None] * freqs[None, :]
    embedded = jnp.concatenate([jnp.cos(angles), jnp.sin(angles)], axis=1)
    gate = jnp.dot(embedded, time_weight.astype(jnp.float32), precision=lax.Precision.HIGHEST)

    results = {}
    for step in far_first + [0]:
        mine = pl.pallas_call(
            functools.partial(attend, (count, listed, half_count), step),
            out_shape=jax.ShapeDtypeStruct((rows, width), jnp.bfloat16),
            in_specs=[SMEM, SMEM, VMEM, VMEM, VMEM],
            out_specs=VMEM,
            name=f"attend_{step}",
        )(where, tile_offsets, gate, asked[step], window)
        results[step] = swap(mine, step) if step else mine
    return pl.pallas_call(
        functools.partial(place_pieces, count),
        out_shape=jax.ShapeDtypeStruct((rows, channels), jnp.bfloat16),
        in_specs=[SMEM] + [VMEM] * count,
        out_specs=pl.BlockSpec(memory_space=pl.ANY),
        scratch_shapes=[pltpu.SemaphoreType.DMA((count,))],
        name="place_pieces",
    )(where, *[results[step] for step in range(count)])


def solution(mesh):
    return jax.shard_map(
        local,
        mesh=mesh,
        in_specs=(
            P(("groups", "span", "head"), None),
            P(("groups", "span", "head"), None),
            P(("groups", "span", "head"), None),
            P(("groups", "span"), None),
            P(("groups", "span")),
            P(None, "head"),
        ),
        out_specs=P(("groups", "span", "head"), None),
        check_vma=False,
    )
```

```python
import functools
import math

import jax
import jax.numpy as jnp
from jax import lax
from jax.experimental import pallas as pl
from jax.experimental.pallas import tpu as pltpu
from jax.sharding import PartitionSpec as P

HEAD_SIZE = 128
TILE = 128
FREQ = 256
KERNEL_VMEM = 16 << 20


def attend(shape, tile_step, offsets_ref, gate_ref, q_ref, window_ref, out_ref):
    count, listed, tail = shape
    width = q_ref.shape[1]
    position, place = lax.axis_index("span"), lax.axis_index("head")
    tile = jnp.bitwise_xor(place, tile_step)
    scale = HEAD_SIZE ** (-0.5)
    slots, usable = [], []
    for j in range(listed):
        source = tile - offsets_ref[tile, j]
        step = jnp.bitwise_xor(jnp.bitwise_and(source, count - 1), place)
        slots.append(
            jnp.where(
                source >= 0,
                tail + count + step,
                jnp.where(source >= -count, tail + step, jnp.bitwise_and(step, tail - 1)),
            )
        )
        usable.append(position * count + source >= 0)
    for h in range(width // HEAD_SIZE):
        cols = slice(h * HEAD_SIZE, (h + 1) * HEAD_SIZE)
        value_cols = slice(width + h * HEAD_SIZE, width + (h + 1) * HEAD_SIZE)
        q = q_ref[:, cols]
        scores = []
        for j in range(listed):
            s = lax.dot_general(
                q, window_ref[slots[j], :, cols], (((1,), (1,)), ((), ())),
                preferred_element_type=jnp.float32,
            )
            scores.append(jnp.where(usable[j], s * scale, -1e30))
        top = functools.reduce(jnp.maximum, scores)
        top = jnp.max(top, axis=1, keepdims=True)
        total = jnp.zeros((TILE, HEAD_SIZE), jnp.float32)
        mixed = jnp.zeros((TILE, HEAD_SIZE), jnp.float32)
        for j in range(listed):
            weights = jnp.exp(scores[j] - top)
            total = total + weights
            mixed = mixed + jnp.dot(
                weights.astype(jnp.bfloat16), window_ref[slots[j], :, value_cols],
                preferred_element_type=jnp.float32,
            )
        total = jnp.sum(total, axis=1, keepdims=True)
        out_ref[:, cols] = (mixed / total * (1.0 + gate_ref[:, cols])).astype(jnp.bfloat16)


def place_pieces(count, *refs):
    pieces, out_ref, sems = refs[:count], refs[count], refs[count + 1]
    width = pieces[0].shape[1]
    copies = []
    for step in range(count):
        column = pl.multiple_of(jnp.bitwise_xor(lax.axis_index("head"), step) * width, width)
        copies.append(
            pltpu.make_async_copy(pieces[step], out_ref.at[:, pl.ds(column, width)], sems.at[step])
        )
        copies[-1].start()
    for copy in copies:
        copy.wait()


SMEM = pl.BlockSpec(memory_space=pltpu.SMEM)
VMEM = pl.BlockSpec(memory_space=pltpu.VMEM)


def local(queries, keys, values, tile_offsets, timesteps, time_weight):
    count = lax.axis_size("head")
    spans = lax.axis_size("span")
    rows, channels = queries.shape
    width = channels // count
    listed = tile_offsets.shape[1]
    half_count = count // 2
    place = lax.axis_index("head")

    def piece(array, step):
        return lax.dynamic_slice(array, (0, (place ^ step) * width), (rows, width))

    def swap(value, step):
        return lax.ppermute(value, "head", [(i, i ^ step) for i in range(count)])

    quarter = max(half_count // 2, 1)
    late = [
        list(range(half_count, half_count + quarter)),
        list(range(half_count + quarter, count)),
    ]
    early = list(range(1, half_count))
    order = late[0] + late[1] + early
    held = {0: jnp.concatenate([piece(keys, 0), piece(values, 0)], axis=1)}
    for step in order:
        held[step] = swap(jnp.concatenate([piece(keys, step), piece(values, step)], axis=1), step)
    asked = {0: piece(queries, 0)}
    after = held[count - 1]
    for step in order:
        asked[step] = swap(lax.optimization_barrier((piece(queries, step), after))[0], step)

    def shifted(value, by):
        return lax.ppermute(value, "span", [(i, i + by) for i in range(spans - by)])

    own = jnp.stack([held[step] for step in [0] + early])
    near, far = [shifted(own, 1)], []
    for group, mate in zip(late, (own[:quarter], own[quarter:])):
        mine = jnp.stack([held[step] for step in group])
        near.append(shifted(mine, 1))
        far.append(shifted(jnp.where(place >= half_count, mate, mine), 2))
        own = jnp.concatenate([own, mine])
    window = jnp.concatenate(far + near + [own], axis=0)

    half = FREQ // 2
    freqs = jnp.exp(-math.log(10000.0) * jnp.arange(half, dtype=jnp.float32) / half)
    angles = timesteps.astype(jnp.float32)[:, None] * freqs[None, :]
    embedded = jnp.concatenate([jnp.cos(angles), jnp.sin(angles)], axis=1)
    gate = jnp.dot(embedded, time_weight.astype(jnp.float32), precision=lax.Precision.HIGHEST)

    results = {}
    for step in order + [0]:
        mine = pl.pallas_call(
            functools.partial(attend, (count, listed, half_count), step),
            out_shape=jax.ShapeDtypeStruct((rows, width), jnp.bfloat16),
            in_specs=[SMEM, VMEM, VMEM, VMEM],
            out_specs=VMEM,
            compiler_params=pltpu.CompilerParams(vmem_limit_bytes=KERNEL_VMEM),
            name=f"attend_{step}",
        )(tile_offsets, gate, asked[step], window)
        results[step] = swap(mine, step) if step else mine
    return pl.pallas_call(
        functools.partial(place_pieces, count),
        out_shape=jax.ShapeDtypeStruct((rows, channels), jnp.bfloat16),
        in_specs=[VMEM] * count,
        compiler_params=pltpu.CompilerParams(vmem_limit_bytes=KERNEL_VMEM),
        out_specs=pl.BlockSpec(memory_space=pl.ANY),
        scratch_shapes=[pltpu.SemaphoreType.DMA((count,))],
        name="place_pieces",
    )(*[results[step] for step in range(count)])


def solution(mesh):
    return jax.shard_map(
        local,
        mesh=mesh,
        in_specs=(
            P(("groups", "span", "head"), None),
            P(("groups", "span", "head"), None),
            P(("groups", "span", "head"), None),
            P(("groups", "span"), None),
            P(("groups", "span")),
            P(None, "head"),
        ),
        out_specs=P(("groups", "span", "head"), None),
        check_vma=False,
    )
```

```python
import functools
import math

import jax
import jax.numpy as jnp
from jax import lax
from jax.experimental import pallas as pl
from jax.experimental.pallas import tpu as pltpu
from jax.sharding import PartitionSpec as P

HEAD_SIZE = 128
TILE = 128
FREQ = 256
KERNEL_VMEM = 16 << 20


def attend(shape, tile_step, offsets_ref, gate_ref, q_ref, window_ref, out_ref):
    count, listed = shape
    width = q_ref.shape[1]
    position, place = lax.axis_index("span"), lax.axis_index("head")
    tile = jnp.bitwise_xor(place, tile_step)
    scale = HEAD_SIZE ** (-0.5) / math.log(2.0)
    slots, usable = [], []
    for j in range(listed):
        source = tile - (j if offsets_ref is None else offsets_ref[tile, j])
        step = jnp.bitwise_xor(jnp.bitwise_and(source, count - 1), place)
        back = jnp.where(source >= 0, 2 * count, jnp.where(source >= -count, count, 0))
        slots.append(back + step)
        usable.append(position * count + source >= 0)
    for h in range(width // HEAD_SIZE):
        cols = slice(h * HEAD_SIZE, (h + 1) * HEAD_SIZE)
        value_cols = slice(width + h * HEAD_SIZE, width + (h + 1) * HEAD_SIZE)
        q = q_ref[:, cols]
        scores = []
        for j in range(listed):
            s = lax.dot_general(
                q, window_ref[slots[j], :, cols], (((1,), (1,)), ((), ())),
                preferred_element_type=jnp.float32,
            )
            scores.append(jnp.where(usable[j], s, -1e30))
        top = functools.reduce(jnp.maximum, scores)
        top = jnp.max(top, axis=1, keepdims=True)
        total = jnp.zeros((TILE, HEAD_SIZE), jnp.float32)
        mixed = jnp.zeros((TILE, HEAD_SIZE), jnp.float32)
        for j in range(listed):
            weights = jnp.exp2((scores[j] - top) * scale)
            total = total + weights
            mixed = mixed + jnp.dot(
                weights.astype(jnp.bfloat16), window_ref[slots[j], :, value_cols],
                preferred_element_type=jnp.float32,
            )
        total = jnp.sum(total, axis=1, keepdims=True)
        out_ref[:, cols] = (mixed / total * (1.0 + gate_ref[:, cols])).astype(jnp.bfloat16)


def place_pieces(count, *refs):
    pieces, out_ref, sems = refs[:count], refs[count], refs[count + 1]
    width = pieces[0].shape[1]
    copies = []
    for step in range(count):
        column = pl.multiple_of(jnp.bitwise_xor(lax.axis_index("head"), step) * width, width)
        copies.append(
            pltpu.make_async_copy(pieces[step], out_ref.at[:, pl.ds(column, width)], sems.at[step])
        )
        copies[-1].start()
    for copy in copies:
        copy.wait()


def exchange_plan(count):
    half = count // 2
    return [(step, "kv") for step in range(1, count)] + [(step, "q") for step in range(1, count)]


SMEM = pl.BlockSpec(memory_space=pltpu.SMEM)
VMEM = pl.BlockSpec(memory_space=pltpu.VMEM)


def local(queries, keys, values, tile_offsets, timesteps, time_weight):
    count = lax.axis_size("head")
    spans = lax.axis_size("span")
    rows, channels = queries.shape
    width = channels // count
    listed = tile_offsets.shape[1]
    half_count = count // 2
    place = lax.axis_index("head")

    def piece(array, step):
        return lax.dynamic_slice(array, (0, (place ^ step) * width), (rows, width))

    def swap(value, step):
        return lax.ppermute(value, "head", [(i, i ^ step) for i in range(count)])

    def packed(step, names):
        parts = [piece(arrays[name], step) for name in names]
        return parts[0] if len(parts) == 1 else jnp.concatenate(parts, axis=1)

    arrays = {"k": keys, "v": values, "q": queries}
    held = {0: packed(0, "kv")}
    asked = {0: packed(0, "q")}
    after = None
    for step, names in exchange_plan(count):
        out = packed(step, names)
        if names == "q" and after is not None:
            out = lax.optimization_barrier((out, after))[0]
        got = swap(out, step)
        if "k" in names:
            held[step] = got[:, : 2 * width]
        if "q" in names:
            asked[step] = got[:, (len(names) - 1) * width :]

    core = lax.rem(lax.axis_index("span"), 2)
    quarter = max(half_count // 2, 1)
    own, far, near = [], [], []
    for low, high in ((0, half_count), (half_count, half_count + quarter), (half_count + quarter, count)):
        mine = jnp.stack([held[step] for step in range(low, high)])
        earlier = lax.ppermute(mine, "span", [(i, (i + 2) % spans) for i in range(spans)])
        passed = jnp.where(core == 0, mine, earlier)
        own.append(mine)
        far.append(earlier)
        near.append(lax.ppermute(passed, "span", [(i, i ^ 1) for i in range(spans)]))
    window = jnp.concatenate(far + near + own, axis=0)

    half = FREQ // 2
    freqs = jnp.exp(-math.log(10000.0) * jnp.arange(half, dtype=jnp.float32) / half)
    angles = timesteps.astype(jnp.float32)[:, None] * freqs[None, :]
    embedded = jnp.concatenate([jnp.cos(angles), jnp.sin(angles)], axis=1)
    gate = jnp.dot(embedded, time_weight.astype(jnp.float32), precision=lax.Precision.HIGHEST)

    dense = listed == count + half_count + 1
    results = {}
    for step in list(range(count - 1, 0, -1)) + [0]:
        mine = pl.pallas_call(
            functools.partial(attend, (count, listed), step)
            if not dense
            else functools.partial(attend, (count, listed), step, None),
            out_shape=jax.ShapeDtypeStruct((rows, width), jnp.bfloat16),
            in_specs=([] if dense else [SMEM]) + [VMEM] * 3,
            out_specs=VMEM,
            compiler_params=pltpu.CompilerParams(vmem_limit_bytes=KERNEL_VMEM),
            name=f"attend_{step}",
        )(*([] if dense else [tile_offsets]), gate, asked[step], window)
        results[step] = swap(mine, step) if step else mine
    return pl.pallas_call(
        functools.partial(place_pieces, count),
        out_shape=jax.ShapeDtypeStruct((rows, channels), jnp.bfloat16),
        in_specs=[VMEM] * count,
        compiler_params=pltpu.CompilerParams(vmem_limit_bytes=KERNEL_VMEM),
        out_specs=pl.BlockSpec(memory_space=pl.ANY),
        scratch_shapes=[pltpu.SemaphoreType.DMA((count,))],
        name="place_pieces",
    )(*[results[step] for step in range(count)])


def solution(mesh):
    return jax.shard_map(
        local,
        mesh=mesh,
        in_specs=(
            P(("groups", "span", "head"), None),
            P(("groups", "span", "head"), None),
            P(("groups", "span", "head"), None),
            P(("groups", "span"), None),
            P(("groups", "span")),
            P(None, "head"),
        ),
        out_specs=P(("groups", "span", "head"), None),
        check_vma=False,
    )
```

```python
import functools
import math

import jax
import jax.numpy as jnp
from jax import lax
from jax.experimental import pallas as pl
from jax.experimental.pallas import tpu as pltpu
from jax.sharding import PartitionSpec as P


HEAD_SIZE = 128
TILE = 128
FREQ = 256
KERNEL_VMEM = 16 << 20
BUFFERS = 3
AHEAD = 1


def attend(shape, steps, offsets_ref, gate_ref, *refs):
    count, listed = shape
    q_refs, window_ref = refs[: len(steps)], refs[len(steps)]
    out_refs, scores_refs = refs[len(steps) + 1 : -BUFFERS], refs[-BUFFERS:]
    width = gate_ref.shape[1]
    position, place = lax.axis_index("span"), lax.axis_index("head")
    first = jnp.right_shift(place, 20)
    scale = HEAD_SIZE ** (-0.5) / math.log(2.0)
    units = [(i, h) for i in range(len(steps)) for h in range(width // HEAD_SIZE)]
    key_slots, value_slots, unusable = [], [], []
    for tile_step in steps:
        tile = jnp.bitwise_xor(place, tile_step)
        home = 2 * count + tile_step
        ks, vs, missing = [], [], jnp.int32(0)
        for j in range(listed):
            source = tile - (j if offsets_ref is None else offsets_ref[tile, j])
            step = jnp.bitwise_xor(jnp.bitwise_and(source, count - 1), place)
            back = jnp.where(source >= 0, 2 * count, jnp.where(source >= -count, count, 0))
            usable = position * count + source >= 0
            ks.append(jnp.where(usable, back + step, home) if j else home)
            vs.append(jnp.where(usable, back + step, 3 * count) if j else home)
            missing = missing + jnp.where(usable, 0, 1)
        key_slots.append(ks)
        value_slots.append(vs)
        unusable.append(missing.astype(jnp.float32))

    def score(u):
        i, h = units[u]
        cols = slice(h * HEAD_SIZE, (h + 1) * HEAD_SIZE)
        q = q_refs[i][:, cols]
        top = None
        for j in range(listed):
            s = lax.dot_general(
                q, window_ref[key_slots[i][j], :, cols], (((1,), (1,)), ((), ())),
                preferred_element_type=jnp.float32,
            )
            scores_refs[u % BUFFERS][0, j] = s
            top = s if top is None else jnp.maximum(top, s)
        return jnp.max(top, axis=1, keepdims=True)

    def mix(u, top):
        i, h = units[u]
        cols = slice(h * HEAD_SIZE, (h + 1) * HEAD_SIZE)
        value_cols = slice(width + h * HEAD_SIZE, width + (h + 1) * HEAD_SIZE)
        total, mixed = None, None
        for j in range(listed):
            weights = jnp.exp2((scores_refs[u % BUFFERS][first, j] - top) * scale)
            total = weights * (1.0 - unusable[i]) if total is None else total + weights
            part = jnp.dot(
                weights.astype(jnp.bfloat16), window_ref[value_slots[i][j], :, value_cols],
                preferred_element_type=jnp.float32,
            )
            mixed = part if mixed is None else mixed + part
        factor = 1.0 / jnp.sum(total, axis=1, keepdims=True)
        out_refs[i][:, cols] = (mixed * factor * (1.0 + gate_ref[:, cols])).astype(jnp.bfloat16)

    tops = {}
    for u in range(len(units) + AHEAD):
        if u < len(units):
            tops[u] = score(u)
        if u >= AHEAD:
            mix(u - AHEAD, tops.pop(u - AHEAD))


def place_pieces(count, *refs):
    pieces, out_ref, sems = refs[:count], refs[count], refs[count + 1]
    width = pieces[0].shape[1]
    copies = []
    for step in range(count):
        column = pl.multiple_of(jnp.bitwise_xor(lax.axis_index("head"), step) * width, width)
        copies.append(
            pltpu.make_async_copy(pieces[step], out_ref.at[:, pl.ds(column, width)], sems.at[step])
        )
        copies[-1].start()
    for copy in copies:
        copy.wait()


SMEM = pl.BlockSpec(memory_space=pltpu.SMEM)
VMEM = pl.BlockSpec(memory_space=pltpu.VMEM)


def local(queries, keys, values, tile_offsets, timesteps, time_weight):
    count = lax.axis_size("head")
    spans = lax.axis_size("span")
    rows, channels = queries.shape
    width = channels // count
    listed = tile_offsets.shape[1]
    half_count = count // 2
    place = lax.axis_index("head")

    def piece(array, step):
        return lax.dynamic_slice(array, (0, (place ^ step) * width), (rows, width))

    def swap(value, step):
        return lax.ppermute(value, "head", [(i, i ^ step) for i in range(count)])

    def shift(value, pairs):
        return lax.ppermute(value, "span", pairs)

    held = {0: jnp.concatenate([piece(keys, 0), piece(values, 0)], axis=1)}
    asked = {0: piece(queries, 0)}
    for step in range(1, count):
        sent = jnp.concatenate([piece(keys, step), piece(values, step)], axis=1)
        held[step] = swap(sent, step)
        asked[step] = swap(piece(queries, step), step)

    core = lax.rem(lax.axis_index("span"), 2)
    chip_on = [(i, (i + 2) % spans) for i in range(spans)]
    other_core = [(i, i ^ 1) for i in range(spans)]
    quarter = max(half_count // 2, 1)
    own, far, near = [], [], []
    bounds = [0, half_count, half_count + quarter, count]
    for low, high in zip(bounds, bounds[1:]):
        mine = jnp.stack([held[step] for step in range(low, high)])
        earlier = shift(mine, chip_on)
        passed = jnp.where(core == 0, mine, earlier)
        own.append(mine)
        far.append(earlier)
        near.append(shift(passed, other_core))
    window = jnp.concatenate(far + near + own + [jnp.zeros_like(own[0][:1])], axis=0)

    half = FREQ // 2
    freqs = jnp.exp(-math.log(10000.0) * jnp.arange(half, dtype=jnp.float32) / half)
    angles = timesteps.astype(jnp.float32)[:, None] * freqs[None, :]
    embedded = jnp.concatenate([jnp.cos(angles), jnp.sin(angles)], axis=1)
    gate = jnp.dot(embedded, time_weight.astype(jnp.float32), precision=lax.Precision.HIGHEST)

    dense = listed == count + half_count + 1
    results = {}
    for steps in [[step] for step in range(count - 1, 1, -1)] + [[1, 0]]:
        kernel = functools.partial(attend, (count, listed), steps)
        found = pl.pallas_call(
            functools.partial(kernel, None) if dense else kernel,
            out_shape=[jax.ShapeDtypeStruct((rows, width), jnp.bfloat16)] * len(steps),
            in_specs=([] if dense else [SMEM]) + [VMEM] * (len(steps) + 2),
            out_specs=[VMEM] * len(steps),
            scratch_shapes=[pltpu.VMEM((1, listed, TILE, TILE), jnp.float32)] * BUFFERS,
            compiler_params=pltpu.CompilerParams(vmem_limit_bytes=KERNEL_VMEM),
        )(*([] if dense else [tile_offsets]), gate, *[asked[step] for step in steps], window)
        for step, mine in zip(steps, found):
            results[step] = swap(mine, step) if step else mine
    return pl.pallas_call(
        functools.partial(place_pieces, count),
        out_shape=jax.ShapeDtypeStruct((rows, channels), jnp.bfloat16),
        in_specs=[VMEM] * count,
        compiler_params=pltpu.CompilerParams(vmem_limit_bytes=KERNEL_VMEM),
        out_specs=pl.BlockSpec(memory_space=pl.ANY),
        scratch_shapes=[pltpu.SemaphoreType.DMA((count,))],
        name="place_pieces",
    )(*[results[step] for step in range(count)])


def solution(mesh):
    return jax.shard_map(
        local,
        mesh=mesh,
        in_specs=(
            P(("groups", "span", "head"), None),
            P(("groups", "span", "head"), None),
            P(("groups", "span", "head"), None),
            P(("groups", "span"), None),
            P(("groups", "span")),
            P(None, "head"),
        ),
        out_specs=P(("groups", "span", "head"), None),
        check_vma=False,
    )
```
